32 devices in a mesh: section: 2 (over x), dp: 4 (over z), tensor: 4 (over y, core).
Axes of the slice: x: 2, y: 2, z: 4, core: 2. Of those that a mesh axis runs over, the one named last changes fastest.
Arguments:
- layer_in: bfloat16 [2, 32, 8192], P('section', 'dp'), may hold values from -6 to 6
- ln_gain: float32 [2, 8192], P('section'), may hold values from 0.25 to 1.75
- ln_bias: float32 [2, 8192], P('section'), may hold values from -2 to 2
- w_up: bfloat16 [2, 8192, 32768], P('section', 'tensor', 'dp'), may hold values from -0.0625 to 0.0625
- b_up: float32 [2, 32768], P('section', 'dp'), may hold values from -3 to 3
- w_down: bfloat16 [2, 32768, 8192], P('section', 'dp', 'tensor'), may hold values from -0.03125 to 0.03125
- b_down: float32 [2, 8192], P('section', 'tensor'), may hold values from -3 to 3
Outputs:
- handed: bfloat16 [2, 32, 8192], P('section', 'dp')
The draws below stay inside these ranges and needn't reach their ends.
All inputs are finite; a program needn't handle non-finite values.
Results may differ from the reference program's by a relative error of at most 0.0042.
Values may be sent and summed in bfloat16 or wider, within the bound.
A program may use at most 192 MiB of HBM per device.

```python
import jax
import jax.numpy as jnp
from jax import lax

D = 8192
FF = 32768
TOKENS = 32
SECTIONS = 2


def block_scale(rng, shape, pieces, smallest, largest):
    level = 1.0
    for axis_at, shards_of in pieces:
        steps = jax.random.uniform(jax.random.fold_in(jax.random.fold_in(rng, 6), axis_at), (shards_of,), jnp.float32, smallest / len(pieces), largest / len(pieces))
        level = level * jnp.repeat(jnp.exp(steps), shape[axis_at] // shards_of).reshape((-1,) + (1,) * (len(shape) - 1 - axis_at))
    return level


def normal_values(rng, extent, width, bound, pieces=(), dtype=jnp.bfloat16):
    array = width * jax.random.normal(rng, extent, jnp.float32)
    if pieces:
        array = array * block_scale(rng, extent, pieces, -0.22, 0.18)
    return jnp.clip(array, -bound, bound).astype(dtype)


def setup_inputs(seed: int = 0) -> dict:
    splits = jax.random.split(jax.random.key(seed), 8)
    layer_in = normal_values(splits[0], (SECTIONS, TOKENS, D), 1.0, 6.0, ((0, 2), (1, 4)))
    ln_gain = jnp.clip(1.0 + 0.15 * jax.random.normal(splits[1], (SECTIONS, D), jnp.float32), 0.25, 1.75)
    ln_bias = normal_values(splits[2], (SECTIONS, D), 0.3, 2.0, ((0, 2),), jnp.float32)
    w_up = normal_values(splits[3], (SECTIONS, D, FF), D ** -0.5, 0.0625, ((0, 2), (1, 4), (2, 4)))
    b_up = normal_values(splits[4], (SECTIONS, FF), 0.5, 3.0, ((0, 2), (1, 4)), jnp.float32)
    w_down = normal_values(splits[5], (SECTIONS, FF, D), FF ** -0.5, 0.03125, ((0, 2), (1, 4), (2, 4)))
    b_down = normal_values(splits[6], (SECTIONS, D), 0.5, 3.0, ((0, 2), (1, 4)), jnp.float32)
    return dict(layer_in=layer_in, ln_gain=ln_gain, ln_bias=ln_bias, w_up=w_up, b_up=b_up, w_down=w_down, b_down=b_down)


def one_section(rows, gain, shift, up_weight, up_bias, down_weight, down_bias):
    values = rows.astype(jnp.float32)
    center = lax.optimization_barrier(jnp.mean(values, axis=1, keepdims=True))
    spread = lax.optimization_barrier(jnp.mean(jnp.square(values - center), axis=1, keepdims=True))
    normed = ((values - center) * jax.lax.rsqrt(spread + 1e-05) * gain + shift).astype(jnp.bfloat16)
    pre = jnp.dot(normed, up_weight, preferred_element_type=jnp.float32) + up_bias
    hidden = jax.nn.gelu(pre, approximate=True).astype(jnp.bfloat16)
    mixed = jnp.dot(hidden, down_weight, preferred_element_type=jnp.float32) + down_bias + values
    return mixed.astype(jnp.bfloat16)

def reference(layer_in, ln_gain, ln_bias, w_up, b_up, w_down, b_down):
    outputs = []
    for section_id in range(layer_in.shape[0]):
        outputs.append(one_section(layer_in[section_id], ln_gain[section_id], ln_bias[section_id], w_up[section_id], b_up[section_id], w_down[section_id], b_down[section_id]))
    stacked = jnp.stack(outputs, axis=0)
    return jnp.roll(stacked, 1, axis=0)
```

```python
import functools

import jax
import jax.numpy as jnp
from jax import lax
from jax.experimental import pallas as pl
from jax.experimental.pallas import tpu as pltpu
from jax.sharding import PartitionSpec as P

MESH = pl.DeviceIdType.MESH
BF = jnp.bfloat16
F32 = jnp.float32
LAG_ACROSS = 3
LAG_GELU = 9
LAG_DOWN = 12


def gelu(v):
    return 0.5 * v * (1.0 + jnp.tanh(0.7978845608028654 * (v + 0.044715 * (v * v * v))))


def kernel(
    sizes,
    x_hbm, gain_hbm, shift_hbm, up_hbm, bup_hbm, down_hbm, bdown_hbm,
    out_hbm,
    x_v, gain_v, shift_v, bup_v, bdown_v,
    up_v, down_v,
    norm_s, norm_r, lhs_v,
    resid_s, resid_r,
    pair_s, pair_r, keep_v,
    across_s, across_r,
    hid_v, acc_v,
    part_s, part_r, fin_v,
    in_sem, up_sem, down_sem,
    norm_ss, norm_rs, resid_ss, resid_rs,
    pair_ss, pair_rs, across_ss, across_rs, hid_ss, hid_rs,
    part_ss, part_rs, fin_ss, fin_rs, own_sem,
):
    n_sec, n_dp, n_t, chunks, slots, rows, width, cw = sizes
    outer = n_t // 2
    half = rows * n_dp // 2
    s = lax.axis_index("section")
    d = lax.axis_index("dp")
    t = lax.axis_index("tensor")
    core = lax.rem(t, 2)
    partner = t + 1 - 2 * core
    offset = pl.multiple_of(t * width, width)
    nxt = lax.rem(s + 1, n_sec)
    prv = lax.rem(s + n_sec - 1, n_sec)

    barrier = pltpu.get_barrier_semaphore()
    for k in range(1, n_dp):
        pl.semaphore_signal(barrier, inc=1, device_id=(s, lax.rem(d + k, n_dp), t), device_id_type=MESH)
    for k in range(1, n_t):
        pl.semaphore_signal(barrier, inc=1, device_id=(s, d, lax.rem(t + k, n_t)), device_id_type=MESH)
    for k in range(n_dp):
        pl.semaphore_signal(barrier, inc=1, device_id=(prv, lax.rem(d + k, n_dp), t), device_id_type=MESH)

    small = [
        pltpu.make_async_copy(x_hbm.at[0], x_v, in_sem.at[0]),
        pltpu.make_async_copy(gain_hbm.at[:, pl.ds(offset, width)], gain_v, in_sem.at[1]),
        pltpu.make_async_copy(shift_hbm.at[:, pl.ds(offset, width)], shift_v, in_sem.at[2]),
        pltpu.make_async_copy(bdown_hbm, bdown_v, in_sem.at[3]),
        pltpu.make_async_copy(bup_hbm, bup_v, in_sem.at[4]),
    ]
    for copy in small:
        copy.start()

    def up_copy(c):
        columns = pl.ds(pl.multiple_of(c * cw, cw), cw)
        return pltpu.make_async_copy(up_hbm.at[0, :, columns], up_v.at[c], up_sem.at[c])

    def down_copy(c):
        lines = pl.ds(pl.multiple_of(c * cw, cw), cw)
        slot = lax.rem(c, slots)
        return pltpu.make_async_copy(down_hbm.at[0, lines, :], down_v.at[slot], down_sem.at[slot])

    def run(count, body):
        def step(i, carry):
            body(i)
            return carry
        lax.fori_loop(0, count, step, 0)

    run(chunks, lambda c: up_copy(c).start())
    run(slots, lambda c: down_copy(c).start())

    for copy in small[:4]:
        copy.wait()
    values = x_v[...].astype(F32)
    center = jnp.mean(values, axis=1, keepdims=True)
    spread = jnp.mean(jnp.square(values - center), axis=1, keepdims=True)
    own = x_v[:, pl.ds(offset, width)].astype(F32)
    normed = (own - center) * lax.rsqrt(spread + 1e-05) * gain_v[...] + shift_v[...]
    norm_s[...] = normed.astype(BF)
    resid_s[...] = own + bdown_v[...]
    pl.semaphore_wait(barrier, 2 * n_dp + n_t - 2)

    def norm_copy(k):
        return pltpu.make_async_remote_copy(
            norm_s, norm_r.at[d], norm_ss.at[k - 1], norm_rs.at[k - 1],
            device_id=(s, lax.rem(d + k, n_dp), t), device_id_type=MESH)

    for k in range(1, n_dp):
        norm_copy(k).start()
    resid_copy = pltpu.make_async_remote_copy(
        resid_s, resid_r, resid_ss, resid_rs, device_id=(nxt, d, t), device_id_type=MESH)
    resid_copy.start()
    norm_own = pltpu.make_async_copy(norm_s, norm_r.at[d], own_sem)
    norm_own.start()
    small[4].wait()
    acc_v[...] = jnp.zeros_like(acc_v)
    norm_own.wait()
    for k in range(1, n_dp):
        norm_copy(k).wait_recv()
    lhs_v[...] = norm_r[...].astype(F32).reshape(n_dp * rows, width).astype(BF)

    def pair_copy(c):
        return pltpu.make_async_remote_copy(
            pair_s.at[c], pair_r.at[c], pair_ss.at[c], pair_rs.at[c],
            device_id=(s, d, partner), device_id_type=MESH)

    def across_copy(c, k):
        return pltpu.make_async_remote_copy(
            across_s.at[c], across_r.at[k - 1, c], across_ss.at[k - 1, c], across_rs.at[k - 1, c],
            device_id=(s, d, lax.rem(t + 2 * k, n_t)), device_id_type=MESH)

    def hid_copy(c):
        return pltpu.make_async_remote_copy(
            hid_v.at[c, core], hid_v.at[c, core], hid_ss.at[c], hid_rs.at[c],
            device_id=(s, d, partner), device_id_type=MESH)

    def up_stage(c):
        up_copy(c).wait()
        pre = jnp.dot(lhs_v[...], up_v[c], preferred_element_type=F32)
        first = core == 0
        pair_s[c] = jnp.where(first, pre[half:], pre[:half]).astype(BF)
        pair_copy(c).start()
        keep_v[c] = jnp.where(first, pre[:half], pre[half:])

    def across_stage(c):
        pair_copy(c).wait_recv()
        both = keep_v[c] + pair_r[c].astype(F32)
        across_s[c] = both.astype(BF)
        for k in range(1, outer):
            across_copy(c, k).start()
        keep_v[c] = both

    def gelu_stage(c):
        total = keep_v[c]
        for k in range(1, outer):
            across_copy(c, k).wait_recv()
            total = total + across_r[k - 1, c].astype(F32)
        total = total + bup_v[:, pl.ds(pl.multiple_of(c * cw, cw), cw)]
        hid_v[c, core] = gelu(total).astype(BF)
        hid_copy(c).start()

    def down_stage(c):
        other = pltpu.make_async_remote_copy(
            hid_v.at[c, 1 - core], hid_v.at[c, 1 - core], hid_ss.at[c], hid_rs.at[c],
            device_id=(s, d, partner), device_id_type=MESH)
        other.wait_recv()
        down_copy(c).wait()
        acc_v[...] += jnp.dot(
            hid_v[c].reshape(2 * half, cw), down_v[lax.rem(c, slots)], preferred_element_type=F32)
        if slots < chunks:
            @pl.when(c + slots < chunks)
            def _():
                down_copy(c + slots).start()

    stages = ((0, up_stage), (LAG_ACROSS, across_stage), (LAG_GELU, gelu_stage), (LAG_DOWN, down_stage))

    def tick(i):
        for lag, stage in stages:
            @pl.when((i >= lag) & (i < lag + chunks))
            def _():
                stage(i - lag)

    run(chunks + LAG_DOWN, tick)

    part_s[...] = acc_v[...].reshape(n_dp, rows, width).astype(BF)

    def part_copy(k):
        target = lax.rem(d + k, n_dp)
        return pltpu.make_async_remote_copy(
            part_s.at[target], part_r.at[k], part_ss.at[k], part_rs.at[k],
            device_id=(nxt, target, t), device_id_type=MESH)

    for k in range(n_dp):
        part_copy(k).start()
    resid_copy.wait_recv()
    total = resid_r[...]
    for k in range(n_dp):
        part_copy(k).wait_recv()
        total = total + part_r[k].astype(F32)
    fin_v[...] = total.astype(BF)

    def fin_copy(k):
        place = out_hbm.at[0, :, pl.ds(offset, width)]
        return pltpu.make_async_remote_copy(
            fin_v, place, fin_ss.at[k - 1], fin_rs.at[k - 1],
            device_id=(s, d, lax.rem(t + k, n_t)), device_id_type=MESH)

    for k in range(1, n_t):
        fin_copy(k).start()
    fin_own = pltpu.make_async_copy(fin_v, out_hbm.at[0, :, pl.ds(offset, width)], own_sem)
    fin_own.start()

    for k in range(1, n_dp):
        norm_copy(k).wait_send()
    resid_copy.wait_send()

    def drain(c):
        pair_copy(c).wait_send()
        for k in range(1, outer):
            across_copy(c, k).wait_send()
        hid_copy(c).wait_send()

    run(chunks, drain)
    for k in range(n_dp):
        part_copy(k).wait_send()
    fin_own.wait()
    for k in range(1, n_t):
        fin_copy(k).wait()


def shards(n_sec, n_dp, n_t, layer_in, ln_gain, ln_bias, w_up, b_up, w_down, b_down):
    rows = layer_in.shape[1]
    width, units = w_up.shape[1], w_up.shape[2]
    cw = 512 if units % 512 == 0 else units
    chunks = units // cw
    slots = min(chunks, 12)
    tokens = rows * n_dp
    half = tokens // 2
    outer = n_t // 2
    peers = max(outer - 1, 1)
    sizes = (n_sec, n_dp, n_t, chunks, slots, rows, width, cw)
    dma = pltpu.SemaphoreType.DMA
    scratch = [
        pltpu.VMEM((rows, layer_in.shape[2]), BF),
        pltpu.VMEM((1, width), F32),
        pltpu.VMEM((1, width), F32),
        pltpu.VMEM((1, units), F32),
        pltpu.VMEM((1, width), F32),
        pltpu.VMEM((chunks, width, cw), BF),
        pltpu.VMEM((slots, cw, width), BF),
        pltpu.VMEM((rows, width), BF),
        pltpu.VMEM((n_dp, rows, width), BF),
        pltpu.VMEM((tokens, width), BF),
        pltpu.VMEM((rows, width), F32),
        pltpu.VMEM((rows, width), F32),
        pltpu.VMEM((chunks, half, cw), BF),
        pltpu.VMEM((chunks, half, cw), BF),
        pltpu.VMEM((chunks, half, cw), F32),
        pltpu.VMEM((chunks, half, cw), BF),
        pltpu.VMEM((peers, chunks, half, cw), BF),
        pltpu.VMEM((chunks, 2, half, cw), BF),
        pltpu.VMEM((tokens, width), F32),
        pltpu.VMEM((n_dp, rows, width), BF),
        pltpu.VMEM((n_dp, rows, width), BF),
        pltpu.VMEM((rows, width), BF),
        dma((5,)), dma((chunks,)), dma((slots,)),
        dma((max(n_dp - 1, 1),)), dma((max(n_dp - 1, 1),)), dma, dma,
        dma((chunks,)), dma((chunks,)),
        dma((peers, chunks)), dma((peers, chunks)),
        dma((chunks,)), dma((chunks,)),
        dma((n_dp,)), dma((n_dp,)),
        dma((n_t - 1,)), dma((n_t - 1,)), dma,
    ]
    return pl.pallas_call(
        functools.partial(kernel, sizes),
        out_shape=jax.ShapeDtypeStruct(layer_in.shape, BF),
        in_specs=[pl.BlockSpec(memory_space=pl.ANY)] * 7,
        out_specs=pl.BlockSpec(memory_space=pl.ANY),
        scratch_shapes=scratch,
        compiler_params=pltpu.CompilerParams(
            collective_id=0, has_side_effects=True, vmem_limit_bytes=67000000),
    )(layer_in, ln_gain, ln_bias, w_up, b_up, w_down, b_down)


def solution(mesh):
    counts = [mesh.shape[name] for name in ("section", "dp", "tensor")]
    return jax.shard_map(
        functools.partial(shards, *counts),
        mesh=mesh,
        in_specs=(
            P("section", "dp", None),
            P("section", None),
            P("section", None),
            P("section", "tensor", "dp"),
            P("section", "dp"),
            P("section", "dp", "tensor"),
            P("section", "tensor"),
        ),
        out_specs=P("section", "dp", None),
        check_vma=False,
    )
```

```python
import functools

import jax
import jax.numpy as jnp
from jax import lax
from jax.experimental import pallas as pl
from jax.experimental.pallas import tpu as pltpu
from jax.sharding import PartitionSpec as P

MESH = pl.DeviceIdType.MESH
BF = jnp.bfloat16
F32 = jnp.float32
LAG_ACROSS = 2
LAG_GELU = 6
LAG_DOWN = 8


def gelu(v):
    return 0.5 * v * (1.0 + jnp.tanh(0.7978845608028654 * (v + 0.044715 * (v * v * v))))


def kernel(
    sizes,
    x_hbm, gain_hbm, shift_hbm, up_hbm, bup_hbm, down_hbm, bdown_hbm,
    out_ref,
    x_v, gain_v, shift_v, bup_v, bdown_v,
    up_v, down_v, col_v,
    norm_s, norm_r, lhs_v,
    resid_s, resid_r,
    pair_s, pair_r, keep_v,
    across_s, across_r,
    hid_v, acc_v,
    part_s, part_r, fin_v,
    in_sem, up_sem, down_sem, col_sem,
    norm_ss, norm_rs, resid_ss, resid_rs,
    pair_ss, pair_rs, across_ss, across_rs, hid_ss, hid_rs,
    part_ss, part_rs, fin_ss, fin_rs, own_sem,
):
    n_sec, n_dp, n_t, chunks, lines, blocks, rows, width, cw = sizes
    outer = n_t // 2
    half = rows * n_dp // 2
    s = lax.axis_index("section")
    d = lax.axis_index("dp")
    t = lax.axis_index("tensor")
    core = lax.rem(t, 2)
    partner = t + 1 - 2 * core
    offset = pl.multiple_of(t * width, width)
    nxt = lax.rem(s + 1, n_sec)
    prv = lax.rem(s + n_sec - 1, n_sec)

    barrier = pltpu.get_barrier_semaphore()
    for k in range(1, n_dp):
        pl.semaphore_signal(barrier, inc=1, device_id=(s, lax.rem(d + k, n_dp), t), device_id_type=MESH)
    for k in range(1, n_t):
        pl.semaphore_signal(barrier, inc=1, device_id=(s, d, lax.rem(t + k, n_t)), device_id_type=MESH)
    pl.semaphore_signal(barrier, inc=1, device_id=(prv, d, t), device_id_type=MESH)

    small = [
        pltpu.make_async_copy(x_hbm.at[0], x_v, in_sem.at[0]),
        pltpu.make_async_copy(gain_hbm.at[:, pl.ds(offset, width)], gain_v, in_sem.at[1]),
        pltpu.make_async_copy(shift_hbm.at[:, pl.ds(offset, width)], shift_v, in_sem.at[2]),
        pltpu.make_async_copy(bdown_hbm, bdown_v, in_sem.at[3]),
        pltpu.make_async_copy(bup_hbm, bup_v, in_sem.at[4]),
    ]
    for copy in small:
        copy.start()

    def up_copy(c):
        columns = pl.ds(pl.multiple_of(c * cw, cw), cw)
        return pltpu.make_async_copy(up_hbm.at[0, :, columns], up_v.at[c], up_sem.at[c])

    def down_copy(c):
        part = pl.ds(pl.multiple_of(c * cw, cw), cw)
        return pltpu.make_async_copy(down_hbm.at[0, part, :], down_v.at[c], down_sem.at[c])

    reuse = blocks == chunks - lines and blocks * cw == width
    col_place = up_v if reuse else col_v

    def col_copy(n):
        part = pl.ds(lines * cw, (chunks - lines) * cw)
        columns = pl.ds(pl.multiple_of(n * cw, cw), cw)
        return pltpu.make_async_copy(down_hbm.at[0, part, columns], col_place.at[n], col_sem.at[n])

    def run(count, body):
        def step(i, carry):
            body(i)
            return carry
        lax.fori_loop(0, count, step, 0)

    run(chunks, lambda c: up_copy(c).start())
    run(lines, lambda c: down_copy(c).start())
    if not reuse:
        run(blocks, lambda n: col_copy(n).start())

    for copy in small[:4]:
        copy.wait()
    values = x_v[...].astype(F32)
    center = jnp.mean(values, axis=1, keepdims=True)
    spread = jnp.mean(jnp.square(values - center), axis=1, keepdims=True)
    own = x_v[:, pl.ds(offset, width)].astype(F32)
    normed = (own - center) * lax.rsqrt(spread + 1e-05) * gain_v[...] + shift_v[...]
    norm_s[...] = normed.astype(BF)
    resid_s[...] = own + bdown_v[...]
    pl.semaphore_wait(barrier, n_dp + n_t - 1)

    def norm_copy(k):
        return pltpu.make_async_remote_copy(
            norm_s, norm_r.at[d], norm_ss.at[k - 1], norm_rs.at[k - 1],
            device_id=(s, lax.rem(d + k, n_dp), t), device_id_type=MESH)

    for k in range(1, n_dp):
        norm_copy(k).start()
    resid_copy = pltpu.make_async_remote_copy(
        resid_s, resid_r, resid_ss, resid_rs, device_id=(nxt, d, t), device_id_type=MESH)
    resid_copy.start()
    norm_own = pltpu.make_async_copy(norm_s, norm_r.at[d], own_sem)
    norm_own.start()
    small[4].wait()
    acc_v[...] = jnp.zeros_like(acc_v)
    norm_own.wait()
    for k in range(1, n_dp):
        norm_copy(k).wait_recv()
    lhs_v[...] = norm_r[...].astype(F32).reshape(n_dp * rows, width).astype(BF)

    def pair_copy(c):
        return pltpu.make_async_remote_copy(
            pair_s.at[c], pair_r.at[c], pair_ss.at[c], pair_rs.at[c],
            device_id=(s, d, partner), device_id_type=MESH)

    def across_copy(c, k):
        return pltpu.make_async_remote_copy(
            across_s.at[c], across_r.at[k - 1, c], across_ss.at[k - 1, c], across_rs.at[k - 1, c],
            device_id=(s, d, lax.rem(t + 2 * k, n_t)), device_id_type=MESH)

    def hid_copy(c):
        return pltpu.make_async_remote_copy(
            hid_v.at[c, core], hid_v.at[c, core], hid_ss.at[c], hid_rs.at[c],
            device_id=(s, d, partner), device_id_type=MESH)

    def up_stage(c):
        up_copy(c).wait()
        pre = jnp.dot(lhs_v[...], up_v[c], preferred_element_type=F32)
        first = core == 0
        pair_s[c] = jnp.where(first, pre[half:], pre[:half]).astype(BF)
        pair_copy(c).start()
        keep_v[c] = jnp.where(first, pre[:half], pre[half:])
        if reuse:
            @pl.when(c < blocks)
            def _():
                col_copy(c).start()

    def across_stage(c):
        pair_copy(c).wait_recv()
        both = keep_v[c] + pair_r[c].astype(F32)
        across_s[c] = both.astype(BF)
        for k in range(1, outer):
            across_copy(c, k).start()
        keep_v[c] = both

    def gelu_stage(c):
        total = keep_v[c]
        for k in range(1, outer):
            across_copy(c, k).wait_recv()
            total = total + across_r[k - 1, c].astype(F32)
        total = total + bup_v[:, pl.ds(pl.multiple_of(c * cw, cw), cw)]
        hid_v[c, core] = gelu(total).astype(BF)
        hid_copy(c).start()

    def hid_wait(c):
        pltpu.make_async_remote_copy(
            hid_v.at[c, 1 - core], hid_v.at[c, 1 - core], hid_ss.at[c], hid_rs.at[c],
            device_id=(s, d, partner), device_id_type=MESH).wait_recv()

    def down_stage(c):
        hid_wait(c)
        down_copy(c).wait()
        acc_v[...] += jnp.dot(
            hid_v[c].reshape(2 * half, cw), down_v[c], preferred_element_type=F32)

    stages = (
        (0, chunks, up_stage),
        (LAG_ACROSS, chunks, across_stage),
        (LAG_GELU, chunks, gelu_stage),
        (LAG_DOWN, lines, down_stage),
    )

    def tick(i):
        for lag, count, stage in stages:
            @pl.when((i >= lag) & (i < lag + count))
            def _():
                stage(i - lag)

    run(max(chunks + LAG_GELU, lines + LAG_DOWN), tick)
    for c in range(lines, chunks):
        hid_wait(c)

    def part_copy(n, k):
        target = lax.rem(d + k, n_dp)
        return pltpu.make_async_remote_copy(
            part_s.at[n, target], part_r.at[n, k], part_ss.at[n, k], part_rs.at[n, k],
            device_id=(nxt, target, t), device_id_type=MESH)

    def place(n):
        return out_ref.at[0, :, pl.ds(pl.multiple_of(offset + n * cw, cw), cw)]

    def fin_copy(n, k):
        return pltpu.make_async_remote_copy(
            fin_v.at[n], place(n), fin_ss.at[n, k - 1], fin_rs.at[n, k - 1],
            device_id=(s, d, lax.rem(t + k, n_t)), device_id_type=MESH)

    for n in range(blocks):
        col_copy(n).wait()
        last = jnp.concatenate([hid_v[c].reshape(2 * half, cw) for c in range(lines, chunks)], axis=1)
        part = acc_v[:, n * cw:(n + 1) * cw] + jnp.dot(last, col_place[n], preferred_element_type=F32)
        part_s[n] = part.reshape(n_dp, rows, cw).astype(BF)
        for k in range(n_dp):
            part_copy(n, k).start()
    resid_copy.wait_recv()
    for n in range(blocks):
        total = resid_r[:, n * cw:(n + 1) * cw]
        for k in range(n_dp):
            part_copy(n, k).wait_recv()
            total = total + part_r[n, k].astype(F32)
        fin_v[n] = total.astype(BF)
        for k in range(1, n_t):
            fin_copy(n, k).start()
        place(n)[...] = total.astype(BF)

    for k in range(1, n_dp):
        norm_copy(k).wait_send()
    resid_copy.wait_send()

    def drain(c):
        pair_copy(c).wait_send()
        for k in range(1, outer):
            across_copy(c, k).wait_send()
        hid_copy(c).wait_send()

    run(chunks, drain)
    for n in range(blocks):
        for k in range(n_dp):
            part_copy(n, k).wait_send()
    for n in range(blocks):
        for k in range(1, n_t):
            fin_copy(n, k).wait()


def shards(n_sec, n_dp, n_t, layer_in, ln_gain, ln_bias, w_up, b_up, w_down, b_down):
    rows = layer_in.shape[1]
    width, units = w_up.shape[1], w_up.shape[2]
    cw = 1024 if units % 1024 == 0 else units
    chunks = units // cw
    blocks = width // cw
    lines = max(chunks - blocks, 0)
    reuse = chunks - lines == blocks
    tokens = rows * n_dp
    half = tokens // 2
    outer = n_t // 2
    peers = max(outer - 1, 1)
    sizes = (n_sec, n_dp, n_t, chunks, lines, blocks, rows, width, cw)
    dma = pltpu.SemaphoreType.DMA
    scratch = [
        pltpu.VMEM((rows, layer_in.shape[2]), BF),
        pltpu.VMEM((1, width), F32),
        pltpu.VMEM((1, width), F32),
        pltpu.VMEM((1, units), F32),
        pltpu.VMEM((1, width), F32),
        pltpu.VMEM((chunks, width, cw), BF),
        pltpu.VMEM((max(lines, 1), cw, width), BF),
        pltpu.VMEM((1, 16, 128) if reuse else (blocks, (chunks - lines) * cw, cw), BF),
        pltpu.VMEM((rows, width), BF),
        pltpu.VMEM((n_dp, rows, width), BF),
        pltpu.VMEM((tokens, width), BF),
        pltpu.VMEM((rows, width), F32),
        pltpu.VMEM((rows, width), F32),
        pltpu.VMEM((chunks, half, cw), BF),
        pltpu.VMEM((chunks, half, cw), BF),
        pltpu.VMEM((chunks, half, cw), F32),
        pltpu.VMEM((chunks, half, cw), BF),
        pltpu.VMEM((peers, chunks, half, cw), BF),
        pltpu.VMEM((chunks, 2, half, cw), BF),
        pltpu.VMEM((tokens, width), F32),
        pltpu.VMEM((blocks, n_dp, rows, cw), BF),
        pltpu.VMEM((blocks, n_dp, rows, cw), BF),
        pltpu.VMEM((blocks, rows, cw), BF),
        dma((5,)), dma((chunks,)), dma((max(lines, 1),)), dma((blocks,)),
        dma((max(n_dp - 1, 1),)), dma((max(n_dp - 1, 1),)), dma, dma,
        dma((chunks,)), dma((chunks,)),
        dma((peers, chunks)), dma((peers, chunks)),
        dma((chunks,)), dma((chunks,)),
        dma((blocks, n_dp)), dma((blocks, n_dp)),
        dma((blocks, n_t - 1)), dma((blocks, n_t - 1)), dma,
    ]
    return pl.pallas_call(
        functools.partial(kernel, sizes),
        out_shape=pltpu.VMEM(layer_in.shape, BF),
        in_specs=[pl.BlockSpec(memory_space=pl.ANY)] * 7,
        out_specs=pl.BlockSpec(memory_space=pltpu.VMEM),
        scratch_shapes=scratch,
        compiler_params=pltpu.CompilerParams(
            collective_id=0, has_side_effects=True, vmem_limit_bytes=63 * 1024 * 1024),
    )(layer_in, ln_gain, ln_bias, w_up, b_up, w_down, b_down)


def solution(mesh):
    counts = [mesh.shape[name] for name in ("section", "dp", "tensor")]
    return jax.shard_map(
        functools.partial(shards, *counts),
        mesh=mesh,
        in_specs=(
            P("section", "dp", None),
            P("section", None),
            P("section", None),
            P("section", "tensor", "dp"),
            P("section", "dp"),
            P("section", "dp", "tensor"),
            P("section", "tensor"),
        ),
        out_specs=P("section", "dp", None),
        check_vma=False,
    )
```
